32 devices in a mesh: range: 4 (over x, core), azimuth: 8 (over z, y).
Axes of the slice: x: 2, y: 2, z: 4, core: 2. Of those that a mesh axis runs over, the one named last changes fastest.
Arguments:
- features: bfloat16 [4, 64, 64, 1024], P(None, None, 'range', 'azimuth'), may hold values from -6 to 6
- state_init: bfloat16 [64, 64, 1024], P(None, 'range', 'azimuth'), may hold values from -3 to 3
- kernel: float32 [64, 3, 3], replicated, may hold values from -2 to 2
- gate_weight: bfloat16 [128, 128], replicated, may hold values from -0.5 to 0.5
- cand_weight: bfloat16 [64, 64], replicated, may hold values from -0.75 to 0.75
- recur_weight: bfloat16 [64, 64], replicated, may hold values from -0.75 to 0.75
- down_weight: bfloat16 [128, 1024], replicated, may hold values from -0.1875 to 0.1875
- owner_map: int32 [4, 8, 4], P('range', 'azimuth'), may hold values from 0 to 3, as said below
- dest_map: int32 [4, 8, 4], P('range', 'azimuth'), may hold values from 0 to 3
- cart_cot: bfloat16 [4, 8, 4, 128, 128], P('range', 'azimuth'), may hold values from -6 to 6
Outputs:
- cart: float32 [4, 8, 4, 128, 128], P('range', 'azimuth')
- grad_features: bfloat16 [4, 64, 64, 1024], P(None, None, 'range', 'azimuth')
- grad_state: float32 [64, 64, 1024], P(None, 'range', 'azimuth')
- grad_kernel: float32 [64, 3, 3], replicated
- grad_gate: float32 [128, 128], replicated
- grad_cand: float32 [64, 64], replicated
- grad_recur: float32 [64, 64], replicated
- grad_down: float32 [128, 1024], replicated
The draws below stay inside these ranges and needn't reach their ends.
Inputs may be any that keep to these rules, and one draw needn't show every extreme that they name: `owner_map`: no tile sends more than 2 of its 4 blocks to one owner; in every azimuth column one owner receives exactly 2 blocks from every tile of the column.
All inputs are finite; a program needn't handle non-finite values.
Results may differ from the reference program's by a relative error of at most 0.0065.
Values may be sent and summed in bfloat16 or wider, within the bound.
No kernel may reach another device: no remote copies, remote signals or barrier semaphores. Data moves between devices by JAX's collectives and lax.ppermute only.
A program may use at most 128 MiB of HBM per device.

```python
import math
import jax
import jax.numpy as jnp
from jax import lax

CHANNELS = 64
COARSE = 128
SLICES = 4
DILATION = 8
BLOCK = 128
RANGE_DEV = 16
AZIM_DEV = 128
RANGE_CELLS = 64
AZIM_CELLS = 1024
BLOCKS_SLICE = 1
BLOCKS = 4
CAPACITY = 2
N_RANGE = 4
N_AZIMUTH = 8


def draw_owner_map(key, part):
    key_full = jax.random.fold_in(key, 11)
    key_rank = jax.random.fold_in(key, 12)
    key_turn = jax.random.fold_in(key, 13)
    full_owner = jax.random.randint(key_full, (1, N_AZIMUTH, 1), 0, N_RANGE).astype(jnp.int32)
    scores = jax.random.randint(key_rank, (N_RANGE, N_AZIMUTH, BLOCKS), 0, 1 << 20).astype(jnp.int32) * BLOCKS + jnp.arange(BLOCKS, dtype=jnp.int32)[None, None, :]
    ranked = jnp.argsort(jnp.argsort(scores, axis=2), axis=2).astype(jnp.int32)
    turned = jax.random.randint(key_turn, (N_RANGE, N_AZIMUTH, 1), 0, N_RANGE - 1).astype(jnp.int32)
    others = (full_owner + 1 + (ranked - CAPACITY + turned) % (N_RANGE - 1)) % N_RANGE
    return jnp.where(ranked < CAPACITY, full_owner, others).astype(jnp.int32)


def touch_ends(array, stream_key, least, largest):
    shape = array.shape
    place = [jax.random.randint(jax.random.fold_in(stream_key, axis), (), 0, shape[axis]) for axis in range(len(shape))]
    array = array.at[tuple(place)].set(least)
    longest = shape.index(max(shape))
    place[longest] = (place[longest] + 1) % shape[longest]
    return array.at[tuple(place)].set(largest)


def steps_of(key, extent, pieces, smallest, top_value):
    def one(position, blocks):
        draws = jax.random.uniform(jax.random.fold_in(jax.random.fold_in(key, 6), position), (blocks,), jnp.float32, smallest / len(pieces), top_value / len(pieces))
        return jnp.repeat(jnp.exp(draws), extent[position] // blocks).reshape((-1,) + (1,) * (len(extent) - position - 1))

    factor_of = one(*pieces[0])
    for cut in pieces[1:]:
        factor_of = factor_of * one(*cut)
    return factor_of


def centred(own_key, shape, spread, limit, shards=(), kind=jnp.bfloat16):
    drawn = spread * jax.random.normal(own_key, shape, jnp.float32)
    if shards:
        drawn = drawn * steps_of(own_key, shape, shards, -0.22, 0.18)
    return jnp.clip(drawn, -limit, limit).astype(kind)


def setup_inputs(seed: int = 0) -> dict:
    key_of = jax.random.split(jax.random.key(seed), 11)
    features = centred(key_of[0], (SLICES, CHANNELS, RANGE_CELLS, AZIM_CELLS), 1.0, 6.0, ((2, 4), (3, 8)))
    state_init = centred(key_of[1], (CHANNELS, RANGE_CELLS, AZIM_CELLS), 0.5, 3.0, ((1, 4), (2, 8)))
    kernel = centred(key_of[2], (CHANNELS, 3, 3), 9 ** -0.5, 2.0, (), jnp.float32)
    gate_weight = centred(key_of[3], (2 * CHANNELS, 2 * CHANNELS), (2 * CHANNELS) ** -0.5, 0.5)
    cand_weight = centred(key_of[4], (CHANNELS, CHANNELS), CHANNELS ** -0.5, 0.75)
    recur_weight = centred(key_of[5], (CHANNELS, CHANNELS), CHANNELS ** -0.5, 0.75)
    down_weight = centred(key_of[6], (COARSE, 16 * CHANNELS), (16 * CHANNELS) ** -0.5, 0.1875)
    owner_map = draw_owner_map(jax.random.fold_in(key_of[10], 71), 0)
    dest_map = touch_ends(jax.random.randint(key_of[8], (N_RANGE, N_AZIMUTH, BLOCKS), 0, BLOCKS), jax.random.fold_in(key_of[8], 1), 0, BLOCKS - 1).astype(jnp.int32)
    cart_cot = centred(key_of[9], (N_RANGE, N_AZIMUTH, BLOCKS, COARSE, BLOCK), 1.0, 6.0, ((0, 4), (1, 8)))
    return dict(features=features, state_init=state_init, kernel=kernel, gate_weight=gate_weight, cand_weight=cand_weight, recur_weight=recur_weight, down_weight=down_weight, owner_map=owner_map, dest_map=dest_map, cart_cot=cart_cot)


def framed(field):
    taller = jnp.pad(field, ((0, 0), (1, 1), (0, 0)))
    return jnp.concatenate([taller[:, :, -DILATION:], taller, taller[:, :, :DILATION]], axis=2)

def depthwise(padded, kernel, tile_rows, tile_cols):
    summed = jnp.zeros((padded.shape[0], tile_rows, tile_cols), jnp.float32)
    for tap_row in range(3):
        for tap_col in range(3):
            window = padded[:, tap_row:tap_row + tile_rows, tap_col * DILATION:tap_col * DILATION + tile_cols]
            summed = summed + kernel[:, tap_row, tap_col][:, None, None] * window.astype(jnp.float32)
    return summed

def kernel_terms(padded, dconv, tile_rows, tile_cols):
    grads = dconv.astype(jnp.float32)
    outer_rows = []
    for tap_row in range(3):
        inner_cols = []
        for tap_col in range(3):
            window = padded[:, tap_row:tap_row + tile_rows, tap_col * DILATION:tap_col * DILATION + tile_cols]
            inner_cols.append(lax.optimization_barrier(jnp.sum(grads * window.astype(jnp.float32), axis=(1, 2))))
        outer_rows.append(jnp.stack(inner_cols, axis=1))
    return jnp.stack(outer_rows, axis=1)

def patches(values, tile_rows, tile_cols):
    channels = values.shape[0]
    shaped = values.reshape(channels, tile_rows // 4, 4, tile_cols // 4, 4).transpose(0, 2, 4, 1, 3)
    return shaped.reshape(16 * channels, tile_rows * tile_cols // 16)

def unpatches(grads, tile_rows, tile_cols):
    channels = grads.shape[0] // 16
    shaped = grads.reshape(channels, 4, 4, tile_rows // 4, tile_cols // 4).transpose(0, 3, 1, 4, 2)
    return shaped.reshape(channels, tile_rows * tile_cols)

def cross_cells(left, right):
    return lax.dot_general(left, right, (((1,), (1,)), ((), ())), preferred_element_type=jnp.float32)

def back_product(weight, grads):
    return lax.dot_general(weight, grads, (((0,), (0,)), ((), ())), preferred_element_type=jnp.float32)

def cell_gates(conv_bf, prior_bf, gate_weight, cand_weight, recur_weight):
    channels = conv_bf.shape[0]
    stacked = jnp.concatenate([conv_bf, prior_bf], axis=0)
    preact = jnp.dot(gate_weight, stacked, preferred_element_type=jnp.float32)
    update = jax.nn.sigmoid(preact[:channels])
    reset = jax.nn.sigmoid(preact[channels:])
    recurrent = jnp.dot(recur_weight, prior_bf, preferred_element_type=jnp.float32)
    candidate = jnp.tanh(jnp.dot(cand_weight, conv_bf, preferred_element_type=jnp.float32) + reset * recurrent)
    return (stacked, update, reset, recurrent, candidate)

def reverse_cell(flow_grad, prior_state, update, reset, recurrent, candidate, gate_weight, cand_weight, recur_weight):
    channels = update.shape[0]
    d_update = flow_grad * (candidate - prior_state)
    d_act = flow_grad * update * (1.0 - candidate * candidate)
    d_recur = d_act * reset
    gate_delta = jnp.concatenate([d_update * update * (1.0 - update), d_act * recurrent * reset * (1.0 - reset)], axis=0).astype(jnp.bfloat16)
    cand_delta = d_act.astype(jnp.bfloat16)
    recur_delta = d_recur.astype(jnp.bfloat16)
    reverse_in = back_product(gate_weight, gate_delta)
    dconv = (reverse_in[:channels] + back_product(cand_weight, cand_delta)).astype(jnp.bfloat16)
    carry = (1.0 - update) * flow_grad + reverse_in[channels:] + back_product(recur_weight, recur_delta)
    return (carry, dconv, gate_delta, cand_delta, recur_delta)

def to_blocks(coarse):
    split = coarse.reshape(COARSE, N_RANGE, RANGE_DEV // 4, N_AZIMUTH, AZIM_DEV // 4).transpose(1, 3, 0, 2, 4)
    return split.reshape(N_RANGE, N_AZIMUTH, COARSE, BLOCKS_SLICE, BLOCK).transpose(0, 1, 3, 2, 4)

def from_blocks(blocks):
    grid = blocks.transpose(0, 1, 3, 2, 4).reshape(N_RANGE, N_AZIMUTH, COARSE, RANGE_DEV // 4, AZIM_DEV // 4)
    return grid.transpose(2, 0, 3, 1, 4).reshape(COARSE, RANGE_CELLS * AZIM_CELLS // 16)

def reference(features, state_init, kernel, gate_weight, cand_weight, recur_weight, down_weight, owner_map, dest_map, cart_cot):
    cell_count = RANGE_CELLS * AZIM_CELLS
    hidden = state_init.reshape(CHANNELS, cell_count).astype(jnp.float32)
    padded_list = []
    conv_list = []
    hidden_list = [hidden]
    block_list = []
    for instant in range(SLICES):
        padded = framed(features[instant])
        conv_bf = depthwise(padded, kernel, RANGE_CELLS, AZIM_CELLS).astype(jnp.bfloat16).reshape(CHANNELS, cell_count)
        stacked, update, reset, recurrent, candidate = cell_gates(conv_bf, hidden.astype(jnp.bfloat16), gate_weight, cand_weight, recur_weight)
        hidden = (1.0 - update) * hidden + update * candidate
        coarse = jnp.dot(down_weight, patches(hidden.astype(jnp.bfloat16), RANGE_CELLS, AZIM_CELLS), preferred_element_type=jnp.float32).astype(jnp.bfloat16)
        block_list.append(to_blocks(coarse))
        padded_list.append(padded)
        conv_list.append(conv_bf)
        hidden_list.append(hidden)
    blocks = jnp.concatenate(block_list, axis=2)
    keys = owner_map * BLOCKS + dest_map
    onehot = (keys[:, :, :, None] == jnp.arange(N_RANGE * BLOCKS, dtype=jnp.int32)[None, None, None, :]).astype(jnp.float32)
    flat = blocks.reshape(N_RANGE, N_AZIMUTH, BLOCKS, COARSE * BLOCK).astype(jnp.float32)
    cartesian = jnp.einsum('rabk,rabx->akx', onehot, flat)
    cartesian = cartesian.reshape(N_AZIMUTH, N_RANGE, BLOCKS, COARSE, BLOCK).transpose(1, 0, 2, 3, 4)
    cot_flat = cart_cot.transpose(1, 0, 2, 3, 4).reshape(N_AZIMUTH, N_RANGE * BLOCKS, COARSE * BLOCK).astype(jnp.float32)
    backed = jnp.einsum('rabk,akx->rabx', onehot, cot_flat).astype(jnp.bfloat16)
    backed = backed.reshape(N_RANGE, N_AZIMUTH, BLOCKS, COARSE, BLOCK)
    carry = jnp.zeros((CHANNELS, cell_count), jnp.float32)
    grad_kernel = jnp.zeros((CHANNELS, 3, 3), jnp.float32)
    grad_gate = jnp.zeros((2 * CHANNELS, 2 * CHANNELS), jnp.float32)
    grad_cand = jnp.zeros((CHANNELS, CHANNELS), jnp.float32)
    grad_recur = jnp.zeros((CHANNELS, CHANNELS), jnp.float32)
    grad_down = jnp.zeros((COARSE, 16 * CHANNELS), jnp.float32)
    grad_list = [None] * SLICES
    flipped = kernel[:, ::-1, ::-1]
    for instant in range(SLICES - 1, -1, -1):
        prior_state = hidden_list[instant]
        prior_bf = prior_state.astype(jnp.bfloat16)
        conv_bf = conv_list[instant]
        stacked, update, reset, recurrent, candidate = cell_gates(conv_bf, prior_bf, gate_weight, cand_weight, recur_weight)
        next_bf = hidden_list[instant + 1].astype(jnp.bfloat16)
        d_coarse = from_blocks(backed[:, :, instant * BLOCKS_SLICE:(instant + 1) * BLOCKS_SLICE])
        grad_down = grad_down + cross_cells(d_coarse, patches(next_bf, RANGE_CELLS, AZIM_CELLS))
        flow_grad = carry + unpatches(back_product(down_weight, d_coarse), RANGE_CELLS, AZIM_CELLS)
        carry, dconv, gate_delta, cand_delta, recur_delta = reverse_cell(flow_grad, prior_state, update, reset, recurrent, candidate, gate_weight, cand_weight, recur_weight)
        grad_gate = grad_gate + cross_cells(gate_delta, stacked)
        grad_cand = grad_cand + cross_cells(cand_delta, conv_bf)
        grad_recur = grad_recur + cross_cells(recur_delta, prior_bf)
        dconv_grid = dconv.reshape(CHANNELS, RANGE_CELLS, AZIM_CELLS)
        grad_kernel = grad_kernel + kernel_terms(padded_list[instant], dconv_grid, RANGE_CELLS, AZIM_CELLS)
        grad_list[instant] = depthwise(framed(dconv_grid), flipped, RANGE_CELLS, AZIM_CELLS).astype(jnp.bfloat16)
    grad_scale = 1.0 / math.sqrt(SLICES * RANGE_CELLS * AZIM_CELLS)
    grad_features = jnp.stack(grad_list, axis=0)
    grad_state = carry.reshape(CHANNELS, RANGE_CELLS, AZIM_CELLS)
    return (cartesian, grad_features, grad_state, grad_kernel * grad_scale, grad_gate * grad_scale, grad_cand * grad_scale, grad_recur * grad_scale, grad_down * grad_scale)
```

```python
import functools
import math

import jax
import jax.numpy as jnp
import numpy as np
from jax import lax
from jax.experimental import pallas as pl
from jax.experimental.pallas import tpu as pltpu
from jax.sharding import PartitionSpec as P

DILATION = 8
LANES = 128
LABEL_ROWS = 16
F32 = jnp.float32
BF16 = jnp.bfloat16
NT = (((1,), (1,)), ((), ()))


def mm(left, right):
    return jnp.dot(left, right, preferred_element_type=F32)


def whole(shape):
    zeros = (0,) * len(shape)
    return pl.BlockSpec(shape, lambda *_: zeros)


def turn(value, shift):
    if isinstance(shift, int):
        shift = shift % LANES
        if shift == 0:
            return value
    return pltpu.roll(value, shift, 1)


def lane_index(shape):
    return lax.broadcasted_iota(jnp.int32, shape, len(shape) - 1)


def regroup(row_groups):
    cells = LANES // row_groups
    table = np.zeros((row_groups * LANES, 4 * LANES), np.float32)
    for group in range(row_groups):
        for col in range(LANES):
            phase, coarse = col % 4, col // 4
            table[group * LANES + col, phase * LANES + group * cells + coarse] = 1.0
    return table


def row_windows(row, edge_low, shift_low, edge_high, shift_high):
    lane = lane_index(row.shape)
    low = jnp.where(lane < DILATION, turn(edge_low, shift_low), turn(row, DILATION))
    high = jnp.where(
        lane >= LANES - DILATION, turn(edge_high, shift_high), turn(row, -DILATION)
    )
    return (low, row, high)


class Framed:
    def __init__(self, rows, body, low, high, top, top_edge, bottom, bottom_edge, step):
        self.rows = rows
        self.refs = (body, low, high, top, top_edge, bottom, bottom_edge)
        self.step = step

    def windows(self, start, size):
        body, low, high, top, top_edge, bottom, bottom_edge = self.refs
        span = pl.ds(start, size)
        edge_low = low[0, span, :].astype(F32)
        edge_high = high[0, span, :].astype(F32)
        base = self.step * (2 * DILATION)
        for row in range(-1, self.rows + 1):
            if 0 <= row < self.rows:
                value = body[0, row, span, :].astype(F32)
                yield row, row_windows(
                    value,
                    edge_low,
                    -DILATION * row,
                    edge_high,
                    LANES - DILATION - DILATION * row,
                )
            else:
                source, corner = (top, top_edge) if row < 0 else (bottom, bottom_edge)
                value = source[0, span, :].astype(F32)
                edge = corner[0, span, :].astype(F32)
                shift_low = (LANES - base) % LANES
                shift_high = (2 * LANES - 2 * DILATION - base) % LANES
                yield row, row_windows(value, edge, shift_low, edge, shift_high)


def depthwise_chunk(framed, start, size, taps, emit):
    sums = {}
    for row, windows in framed.windows(start, size):
        for above in range(3):
            target = row + 1 - above
            if not 0 <= target < framed.rows:
                continue
            for side in range(3):
                term = taps[3 * above + side] * windows[side]
                sums[target] = sums[target] + term if target in sums else term
        if row - 1 >= 0:
            emit(row - 1, sums.pop(row - 1))


def tap_columns(kernel_ref, start, size, flip):
    block = kernel_ref[pl.ds(start, size), :]
    order = [8 - tap if flip else tap for tap in range(9)]
    return [jnp.broadcast_to(block[:, tap : tap + 1], (size, LANES)) for tap in order]


def edge_columns(row_of, rows):
    low = high = None
    for row in range(rows):
        value = row_of(row)
        slot = lane_index(value.shape) // DILATION == row
        to_low = turn(value, DILATION * row)
        to_high = turn(value, DILATION * row + DILATION)
        low = jnp.where(slot, to_low, 0.0 if low is None else low)
        high = jnp.where(slot, to_high, 0.0 if high is None else high)
    return low.astype(BF16), high.astype(BF16)


def split_kernel(x_ref, rows_ref, low_ref, high_ref, flat):
    channels, rows = x_ref.shape[1], x_ref.shape[2]
    flat[...] = x_ref[0].reshape(channels * rows, LANES).astype(F32)

    def row_of(row):
        value = flat[pl.ds(row, channels, stride=rows), :]
        rows_ref[0, row] = value.astype(BF16)
        return value

    low_ref[0], high_ref[0] = edge_columns(row_of, rows)


def start_kernel(state_ref, table_ref, out_ref, flat):
    channels, rows = state_ref.shape[0], state_ref.shape[1]
    flat[...] = state_ref[...].reshape(channels * rows, LANES).astype(F32)
    for phase in range(4):
        parts = [
            flat[pl.ds(row, channels, stride=rows), :].astype(BF16)
            for row in range(phase, rows, 4)
        ]
        out_ref[phase * channels : (phase + 1) * channels, :] = mm(
            jnp.concatenate(parts, axis=1), table_ref[...]
        )


def message_kernel(first_ref, last_ref, low_ref, high_ref, down_ref, up_ref):
    slices = first_ref.shape[0]
    corner_down = corner_up = jnp.zeros(first_ref.shape[2:], F32)
    for step in range(slices):
        down_ref[step] = last_ref[step, 0]
        up_ref[step] = first_ref[step, 0]
        base = 2 * DILATION * step
        low = low_ref[step].astype(F32)
        high = high_ref[step].astype(F32)
        slot = lane_index(low.shape) // DILATION
        corner_down = jnp.where(slot == 2 * step, turn(low, base + DILATION), corner_down)
        corner_down = jnp.where(
            slot == 2 * step + 1, turn(high, base + 2 * DILATION), corner_down
        )
        corner_up = jnp.where(slot == 2 * step, turn(low, base), corner_up)
        corner_up = jnp.where(slot == 2 * step + 1, turn(high, base + DILATION), corner_up)
    down_ref[slices] = corner_down.astype(BF16)
    up_ref[slices] = corner_up.astype(BF16)


def forward_kernel(
    capacity,
    scale,
    owner_ref,
    dest_ref,
    x_ref,
    low_ref,
    high_ref,
    top_ref,
    top_edge_ref,
    bottom_ref,
    bottom_edge_ref,
    start_ref,
    kernel_ref,
    table_ref,
    weight_ref,
    down_ref,
    back_ref,
    out_ref,
    keep_ref,
    stack_ref,
    grad_down_ref,
    state,
    conv,
    patch,
):
    step = pl.program_id(0)
    slices = pl.num_programs(0)
    rows, channels = x_ref.shape[1], x_ref.shape[2]
    framed = Framed(
        rows,
        x_ref,
        low_ref,
        high_ref,
        top_ref,
        top_edge_ref,
        bottom_ref,
        bottom_edge_ref,
        step,
    )

    @pl.when(step == 0)
    def _():
        state[...] = start_ref[...]
        grad_down_ref[...] = jnp.zeros_like(grad_down_ref)
        out_ref[:, LANES:, :] = jnp.zeros_like(out_ref[:, LANES:, :])

    size = 16

    def conv_chunk(index, carry):
        start = pl.multiple_of(index * size, size)
        taps = tap_columns(kernel_ref, start, size, False)

        def emit(row, value):
            conv[row, pl.ds(start, size), :] = value.astype(BF16)

        depthwise_chunk(framed, start, size, taps, emit)
        return carry

    lax.fori_loop(0, channels // size, conv_chunk, 0)
    wide = jnp.concatenate(
        [
            jnp.concatenate([conv[row] for row in range(phase, rows, 4)], axis=1)
            for phase in range(4)
        ],
        axis=0,
    )
    grouped = mm(wide, table_ref[...]).astype(BF16)
    for phase in range(4):
        own = slice(phase * channels, (phase + 1) * channels)
        prior = state[own, :]
        stacked = jnp.concatenate([grouped[own], prior.astype(BF16)], axis=0)
        stack_ref[0, phase] = stacked
        pre = mm(weight_ref[...], stacked)
        signed_update = jnp.tanh(0.5 * pre[:channels])
        signed_reset = jnp.tanh(0.5 * pre[channels : 2 * channels])
        update = 0.5 + 0.5 * signed_update
        stay = 0.5 - 0.5 * signed_update
        reset = 0.5 + 0.5 * signed_reset
        recurrent = pre[3 * channels :]
        candidate = jnp.tanh(pre[2 * channels : 3 * channels] + reset * recurrent)
        following = stay * prior + update * candidate
        state[own, :] = following
        act = update * (1.0 - candidate * candidate)
        act_reset = act * reset
        keep_ref[0, 0, own, :] = (candidate - prior) * update * stay
        keep_ref[0, 1, own, :] = act_reset * recurrent * (0.5 - 0.5 * signed_reset)
        keep_ref[0, 2, own, :] = act
        keep_ref[0, 3, own, :] = act_reset
        keep_ref[0, 4, own, :] = stay
        rounded = following.astype(BF16).astype(F32)
        for col in range(4):
            patch[pl.ds(4 * phase + col, channels, stride=16), :] = rounded[
                :, col * LANES : (col + 1) * LANES
            ]
    patched = patch[...].astype(BF16)
    owner = owner_ref[step]
    position = jnp.int32(0)
    for earlier in range(owner_ref.shape[0]):
        position += jnp.where((earlier < step) & (owner_ref[earlier] == owner), 1, 0)
    slot = jnp.minimum(owner * capacity + position, out_ref.shape[0] - 1)
    out_ref[slot, :LANES, :] = mm(down_ref[...], patched).astype(BF16)
    label = (dest_ref[step] + 1).astype(F32)
    out_ref[slot, LANES:, :] = jnp.full((LABEL_ROWS, LANES), label, F32).astype(BF16)
    grad_down_ref[...] += lax.dot_general(
        back_ref[0], patched, NT, preferred_element_type=F32
    )

    @pl.when(step == slices - 1)
    def _():
        grad_down_ref[...] = grad_down_ref[...] * scale


def backward_kernel(
    scale,
    owner_ref,
    dest_ref,
    x_ref,
    low_ref,
    high_ref,
    top_ref,
    top_edge_ref,
    bottom_ref,
    bottom_edge_ref,
    keep_ref,
    stack_ref,
    back_ref,
    table_ref,
    weight_ref,
    down_ref,
    rows_ref,
    edge_low_ref,
    edge_high_ref,
    grad_state_ref,
    small_ref,
    carry,
    patch,
    dense,
    taps,
    flat,
):
    turn_index = pl.program_id(0)
    slices = pl.num_programs(0)
    step = slices - 1 - turn_index
    rows, channels = x_ref.shape[1], x_ref.shape[2]
    groups = rows // 4

    @pl.when(turn_index == 0)
    def _():
        carry[...] = jnp.zeros_like(carry)
        dense[...] = jnp.zeros_like(dense)
        taps[...] = jnp.zeros_like(taps)

    patch[...] = mm(down_ref[...], back_ref[0])
    flat_grads = []
    for phase in range(4):
        own = slice(phase * channels, (phase + 1) * channels)
        unpatched = jnp.concatenate(
            [patch[pl.ds(4 * phase + col, channels, stride=16), :] for col in range(4)], axis=1
        )
        flow = carry[own, :] + unpatched
        delta = jnp.concatenate(
            [(flow * keep_ref[0, part, own, :]).astype(BF16) for part in range(4)], axis=0
        )
        reverse = mm(weight_ref[...], delta)
        carry[own, :] = keep_ref[0, 4, own, :] * flow + reverse[channels:]
        flat_grads.append(reverse[:channels].astype(BF16))
        dense[...] += lax.dot_general(
            delta, stack_ref[0, phase], NT, preferred_element_type=F32
        )
    spread = mm(jnp.concatenate(flat_grads, axis=0), table_ref[...])

    def row_of(row):
        group, phase = row // 4, row % 4
        value = spread[
            phase * channels : (phase + 1) * channels, group * LANES : (group + 1) * LANES
        ]
        rows_ref[0, row] = value.astype(BF16)
        return value

    edge_low_ref[0], edge_high_ref[0] = edge_columns(row_of, rows)
    framed = Framed(
        rows,
        x_ref,
        low_ref,
        high_ref,
        top_ref,
        top_edge_ref,
        bottom_ref,
        bottom_edge_ref,
        step,
    )
    size = 16

    def tap_chunk(index, loop_carry):
        start = pl.multiple_of(index * size, size)
        span = pl.ds(start, size)
        sums = [taps[tap, span, :] for tap in range(9)]
        for row, windows in framed.windows(start, size):
            for above in range(3):
                target = row + 1 - above
                if not 0 <= target < rows:
                    continue
                grad = rows_ref[0, target, span, :].astype(F32)
                for side in range(3):
                    sums[3 * above + side] = sums[3 * above + side] + grad * windows[side]
        for tap in range(9):
            taps[tap, span, :] = sums[tap]
        return loop_carry

    lax.fori_loop(0, channels // size, tap_chunk, 0)

    @pl.when(turn_index == slices - 1)
    def _():
        remain = carry[...]
        total = None
        for _part in range(3):
            piece = remain.astype(BF16)
            remain = remain - piece.astype(F32)
            term = mm(piece, table_ref[...])
            total = term if total is None else total + term
        for phase in range(4):
            for group in range(groups):
                flat[pl.ds(4 * group + phase, channels, stride=rows), :] = total[
                    phase * channels : (phase + 1) * channels,
                    group * LANES : (group + 1) * LANES,
                ]
        grad_state_ref[...] = flat[...].reshape(channels, rows, LANES)
        small_ref[: 2 * channels, :] = dense[: 2 * channels, :] * scale
        lower = dense[2 * channels : 3 * channels, :]
        upper = dense[3 * channels :, :]
        small_ref[2 * channels : 3 * channels, :] = (
            jnp.where(lane_index(lower.shape) < channels, lower, upper) * scale
        )
        gathered = jnp.zeros((channels, LANES), F32)
        for tap in range(9):
            column = jnp.sum(taps[tap], axis=1, keepdims=True)
            gathered = jnp.where(lane_index(gathered.shape) == tap, column, gathered)
        small_ref[3 * channels :, :] = jnp.concatenate(
            [gathered.T[:16] * scale, jnp.zeros((16, LANES - channels), F32)], axis=1
        )


def features_kernel(
    x_ref,
    low_ref,
    high_ref,
    top_ref,
    top_edge_ref,
    bottom_ref,
    bottom_edge_ref,
    kernel_ref,
    out_ref,
    flat,
):
    step = pl.program_id(0)
    rows, channels = x_ref.shape[1], x_ref.shape[2]
    framed = Framed(
        rows,
        x_ref,
        low_ref,
        high_ref,
        top_ref,
        top_edge_ref,
        bottom_ref,
        bottom_edge_ref,
        step,
    )
    size = 16

    def conv_chunk(index, carry):
        start = pl.multiple_of(index * size, size)
        taps = tap_columns(kernel_ref, start, size, True)

        def emit(row, value):
            flat[pl.ds(start * rows + row, size, stride=rows), :] = value

        depthwise_chunk(framed, start, size, taps, emit)
        return carry

    lax.fori_loop(0, channels // size, conv_chunk, 0)
    out_ref[0] = flat[...].reshape(channels, rows, LANES).astype(BF16)


def landing_kernel(blocks, arrived_ref, out_ref):
    for dest in range(blocks):
        total = jnp.zeros(out_ref.shape[1:], F32)
        for slot in range(arrived_ref.shape[0]):
            label = arrived_ref[slot, LANES : LANES + LABEL_ROWS, :].astype(F32)[:1]
            value = arrived_ref[slot, :LANES, :].astype(F32)
            total = total + jnp.where(label == dest + 1, value, 0.0)
        out_ref[dest] = total


def finish_kernel(own_ref, other_ref, gate_ref, cand_ref, recur_ref, taps_ref):
    channels = cand_ref.shape[0]
    total = own_ref[...] + other_ref[...]
    gate_ref[...] = total[: 2 * channels]
    cand_ref[...] = total[2 * channels : 3 * channels, :channels]
    recur_ref[...] = total[2 * channels : 3 * channels, channels:]
    taps_ref[...] = total[3 * channels :, :channels].T


def shifted(value, axis, distance, periodic):
    count = lax.axis_size(axis)
    pairs = [(i, i + 1) for i in range(count - 1)]
    if periodic:
        pairs.append((count - 1, 0))
    if distance < 0:
        pairs = [(target, source) for source, target in pairs]
    return lax.ppermute(value, axis, pairs)


def frame_specs(slices, rows, channels, at):
    return [
        pl.BlockSpec((1, rows, channels, LANES), lambda i, *_: (at(i), 0, 0, 0)),
        pl.BlockSpec((1, channels, LANES), lambda i, *_: (at(i), 0, 0)),
        pl.BlockSpec((1, channels, LANES), lambda i, *_: (at(i), 0, 0)),
        pl.BlockSpec((1, channels, LANES), lambda i, *_: (at(i), 0, 0)),
        pl.BlockSpec((1, channels, LANES), lambda i, *_: (slices, 0, 0)),
        pl.BlockSpec((1, channels, LANES), lambda i, *_: (at(i), 0, 0)),
        pl.BlockSpec((1, channels, LANES), lambda i, *_: (slices, 0, 0)),
    ]


def exchange(rows_array, edge_low, edge_high):
    slices, rows, channels, _ = rows_array.shape
    low = shifted(edge_high, "azimuth", 1, True)
    high = shifted(edge_low, "azimuth", -1, True)
    message = jax.ShapeDtypeStruct((slices + 1, channels, LANES), BF16)
    row_block = (slices, 1, channels, LANES)
    down, up = pl.pallas_call(
        message_kernel,
        grid=(1,),
        in_specs=[
            pl.BlockSpec(row_block, lambda i: (0, 0, 0, 0)),
            pl.BlockSpec(row_block, lambda i: (0, rows - 1, 0, 0)),
            whole(low.shape),
            whole(high.shape),
        ],
        out_specs=[whole(message.shape)] * 2,
        out_shape=[message] * 2,
        name="message",
        cost_estimate=pl.CostEstimate(flops=1, bytes_accessed=1 << 20, transcendentals=0),
    )(rows_array, rows_array, low, high)
    top = shifted(down, "range", 1, False)
    bottom = shifted(up, "range", -1, False)
    return (rows_array, low, high, top, top, bottom, bottom)


def butterfly(value):
    pending = None
    for axis in ("range", "azimuth"):
        count = lax.axis_size(axis)
        gap = 1
        while gap < count:
            if pending is not None:
                value = value + pending
            pending = lax.ppermute(value, axis, [(i, i ^ gap) for i in range(count)])
            gap *= 2
    return value, pending


def on_device(
    features,
    state_init,
    kernel,
    gate_weight,
    cand_weight,
    recur_weight,
    down_weight,
    owner_map,
    dest_map,
    cart_cot,
):
    slices, channels, rows, cols = features.shape
    coarse_ch = down_weight.shape[0]
    ranks = lax.axis_size("range")
    sectors = lax.axis_size("azimuth")
    blocks = owner_map.shape[2]
    capacity = blocks // 2
    assert cols == LANES and rows * cols // 16 == LANES and blocks == slices
    scale = 1.0 / math.sqrt(slices * rows * cols * ranks * sectors)
    table = regroup(rows // 4)
    owners = owner_map.reshape(blocks)
    dests = dest_map.reshape(blocks)
    flat_scratch = pltpu.VMEM((channels * rows, LANES), F32)
    row_shape = jax.ShapeDtypeStruct((slices, rows, channels, LANES), BF16)
    edge_shape = jax.ShapeDtypeStruct((slices, channels, LANES), BF16)
    row_spec = pl.BlockSpec((1, rows, channels, LANES), lambda i, *_: (i, 0, 0, 0))
    edge_spec = pl.BlockSpec((1, channels, LANES), lambda i, *_: (i, 0, 0))
    arranged, edge_low, edge_high = pl.pallas_call(
        split_kernel,
        grid=(slices,),
        in_specs=[pl.BlockSpec((1, channels, rows, LANES), lambda i: (i, 0, 0, 0))],
        out_specs=[row_spec, edge_spec, edge_spec],
        out_shape=[row_shape, edge_shape, edge_shape],
        scratch_shapes=[flat_scratch],
        name="split",
        cost_estimate=pl.CostEstimate(flops=1, bytes_accessed=3 << 20, transcendentals=0),
    )(features)
    frame = exchange(arranged, edge_low, edge_high)

    cot = cart_cot.reshape(blocks, coarse_ch, LANES)
    cots = lax.all_to_all(
        jnp.broadcast_to(cot[None], (ranks,) + cot.shape), "range", 0, 0, tiled=True
    ).reshape(ranks * blocks, coarse_ch, LANES)

    group = (4 * channels, 4 * LANES)
    start = pl.pallas_call(
        start_kernel,
        in_specs=[pl.BlockSpec(memory_space=pltpu.VMEM)] * 2,
        out_specs=pl.BlockSpec(memory_space=pltpu.VMEM),
        out_shape=jax.ShapeDtypeStruct(group, F32),
        scratch_shapes=[flat_scratch],
        name="start",
        cost_estimate=pl.CostEstimate(flops=1 << 27, bytes_accessed=1 << 20, transcendentals=0),
    )(state_init, jnp.asarray(table, BF16))
    empty = jnp.zeros((channels, channels), BF16)
    weight = jnp.concatenate(
        [
            gate_weight,
            jnp.concatenate([cand_weight, empty], axis=1),
            jnp.concatenate([empty, recur_weight], axis=1),
        ],
        axis=0,
    )
    taps = kernel.reshape(channels, 9)
    back_spec = lambda at: pl.BlockSpec(
        (1, coarse_ch, LANES), lambda i, own, dst: (own[at(i)] * blocks + dst[at(i)], 0, 0)
    )
    ahead = lambda i: i
    behind = lambda i: slices - 1 - i
    out_blocks = jax.ShapeDtypeStruct((ranks * capacity, coarse_ch + LABEL_ROWS, LANES), BF16)
    keep_shape = jax.ShapeDtypeStruct((slices, 5) + group, F32)
    stack_shape = jax.ShapeDtypeStruct((slices, 4, 2 * channels, 4 * LANES), BF16)
    down_shape = jax.ShapeDtypeStruct(down_weight.shape, F32)
    keep_spec = lambda at: pl.BlockSpec((1, 5) + group, lambda i, *_: (at(i), 0, 0, 0))
    stack_spec = lambda at: pl.BlockSpec(
        (1, 4, 2 * channels, 4 * LANES), lambda i, *_: (at(i), 0, 0, 0)
    )
    outgoing, keep, stack, grad_down = pl.pallas_call(
        functools.partial(forward_kernel, capacity, scale),
        grid_spec=pltpu.PrefetchScalarGridSpec(
            num_scalar_prefetch=2,
            grid=(slices,),
            in_specs=frame_specs(slices, rows, channels, ahead)
            + [
                whole(group),
                whole(taps.shape),
                whole(table.shape),
                whole(weight.shape),
                whole(down_weight.shape),
                back_spec(ahead),
            ],
            out_specs=[
                whole(out_blocks.shape),
                keep_spec(ahead),
                stack_spec(ahead),
                whole(down_shape.shape),
            ],
            scratch_shapes=[
                pltpu.VMEM(group, F32),
                pltpu.VMEM((rows, channels, LANES), BF16),
                pltpu.VMEM((16 * channels, LANES), F32),
            ],
        ),
        out_shape=[out_blocks, keep_shape, stack_shape, down_shape],
        name="forward",
        cost_estimate=pl.CostEstimate(flops=1 << 30, bytes_accessed=16 << 20, transcendentals=0),
    )(
        owners,
        dests,
        *frame,
        start,
        taps,
        jnp.asarray(table, BF16),
        weight,
        down_weight,
        cots,
    )

    arrived = lax.all_to_all(
        outgoing.reshape((ranks, capacity) + outgoing.shape[1:]), "range", 0, 0, tiled=True
    ).reshape(outgoing.shape)
    shares = ranks * sectors
    sent = grad_down.astype(BF16).reshape(shares, coarse_ch * 16 * channels // (shares * LANES), LANES)
    pieces = lax.all_to_all(sent, ("range", "azimuth"), 0, 0, tiled=True)
    piece = jnp.sum(pieces.astype(F32), axis=0).astype(BF16)

    rows_grad, low_grad, high_grad, grad_state, small = pl.pallas_call(
        functools.partial(backward_kernel, scale),
        grid_spec=pltpu.PrefetchScalarGridSpec(
            num_scalar_prefetch=2,
            grid=(slices,),
            in_specs=frame_specs(slices, rows, channels, behind)
            + [
                keep_spec(behind),
                stack_spec(behind),
                back_spec(behind),
                whole(table.T.shape),
                whole(weight.T.shape),
                whole(down_weight.T.shape),
            ],
            out_specs=[
                pl.BlockSpec((1, rows, channels, LANES), lambda i, *_: (behind(i), 0, 0, 0)),
                pl.BlockSpec((1, channels, LANES), lambda i, *_: (behind(i), 0, 0)),
                pl.BlockSpec((1, channels, LANES), lambda i, *_: (behind(i), 0, 0)),
                whole((channels, rows, LANES)),
                whole((3 * channels + 16, LANES)),
            ],
            scratch_shapes=[
                pltpu.VMEM(group, F32),
                pltpu.VMEM((16 * channels, LANES), F32),
                pltpu.VMEM((4 * channels, 2 * channels), F32),
                pltpu.VMEM((9, channels, LANES), F32),
                flat_scratch,
            ],
        ),
        out_shape=[
            row_shape,
            edge_shape,
            edge_shape,
            jax.ShapeDtypeStruct((channels, rows, LANES), F32),
            jax.ShapeDtypeStruct((3 * channels + 16, LANES), F32),
        ],
        name="backward",
        cost_estimate=pl.CostEstimate(flops=1 << 30, bytes_accessed=16 << 20, transcendentals=0),
    )(
        owners,
        dests,
        *frame,
        keep,
        stack,
        cots,
        jnp.asarray(table.T, BF16),
        weight.T,
        down_weight.T,
    )

    cartesian = pl.pallas_call(
        functools.partial(landing_kernel, blocks),
        in_specs=[pl.BlockSpec(memory_space=pltpu.VMEM)],
        out_specs=pl.BlockSpec(memory_space=pltpu.VMEM),
        out_shape=jax.ShapeDtypeStruct((blocks, coarse_ch, LANES), F32),
        name="landing",
        cost_estimate=pl.CostEstimate(flops=1, bytes_accessed=1 << 19, transcendentals=0),
    )(arrived)
    spread = lax.all_to_all(
        jnp.broadcast_to(piece[None], sent.shape), ("range", "azimuth"), 0, 0, tiled=True
    )
    grad_down = spread.astype(F32).reshape(down_weight.shape)

    frame_grad = exchange(rows_grad, low_grad, high_grad)
    grad_features = pl.pallas_call(
        features_kernel,
        grid=(slices,),
        in_specs=frame_specs(slices, rows, channels, ahead) + [whole(taps.shape)],
        out_specs=pl.BlockSpec((1, channels, rows, LANES), lambda i: (i, 0, 0, 0)),
        out_shape=jax.ShapeDtypeStruct(features.shape, BF16),
        scratch_shapes=[flat_scratch],
        name="features",
        cost_estimate=pl.CostEstimate(flops=1 << 25, bytes_accessed=4 << 20, transcendentals=0),
    )(*frame_grad, taps)

    own, other = butterfly(small)
    grad_gate, grad_cand, grad_recur, grad_taps = pl.pallas_call(
        finish_kernel,
        in_specs=[pl.BlockSpec(memory_space=pltpu.VMEM)] * 2,
        out_specs=[pl.BlockSpec(memory_space=pltpu.VMEM)] * 4,
        out_shape=[
            jax.ShapeDtypeStruct((2 * channels, 2 * channels), F32),
            jax.ShapeDtypeStruct((channels, channels), F32),
            jax.ShapeDtypeStruct((channels, channels), F32),
            jax.ShapeDtypeStruct((channels, 16), F32),
        ],
        name="finish",
        cost_estimate=pl.CostEstimate(flops=1, bytes_accessed=1 << 18, transcendentals=0),
    )(own, other)
    return (
        cartesian.reshape(cart_cot.shape),
        grad_features,
        grad_state,
        grad_taps[:, :9].reshape(channels, 3, 3),
        grad_gate,
        grad_cand,
        grad_recur,
        grad_down,
    )


def solution(mesh):
    placed = (
        P(None, None, "range", "azimuth"),
        P(None, "range", "azimuth"),
        P(),
        P(),
        P(),
        P(),
        P(),
        P("range", "azimuth", None),
        P("range", "azimuth", None),
        P("range", "azimuth", None, None, None),
    )
    return jax.shard_map(
        on_device,
        mesh=mesh,
        in_specs=placed,
        out_specs=(
            P("range", "azimuth", None, None, None),
            P(None, None, "range", "azimuth"),
            P(None, "range", "azimuth"),
            P(),
            P(),
            P(),
            P(),
            P(),
        ),
        check_vma=False,
    )
```

```python
import functools
import math

import jax
import jax.numpy as jnp
from jax import lax
from jax.experimental import pallas as pl
from jax.experimental.pallas import tpu as pltpu
from jax.sharding import PartitionSpec as P


DILATION = 8
LANES = 128
LABEL_ROWS = 16
CHUNK = 16
F32 = jnp.float32
BF16 = jnp.bfloat16
NT = (((1,), (1,)), ((), ()))
VMEM = pl.BlockSpec(memory_space=pltpu.VMEM)
HBM = pl.BlockSpec(memory_space=pltpu.HBM)
SMEM = pl.BlockSpec(memory_space=pltpu.SMEM)


def mm(left, right):
    return jnp.dot(left, right, preferred_element_type=F32)


def mm_back(left, right):
    return lax.dot_general(left, right, NT, preferred_element_type=F32)


def turn(value, shift):
    if isinstance(shift, int):
        shift = shift % LANES
        if shift == 0:
            return value
    return pltpu.roll(value, shift, 1)


def lane_index(shape):
    return lax.broadcasted_iota(jnp.int32, shape, len(shape) - 1)


def regroup(row_groups):
    cells = LANES // row_groups
    shape = (row_groups * LANES, 4 * LANES)
    raw = lax.broadcasted_iota(jnp.int32, shape, 0)
    grouped = lax.broadcasted_iota(jnp.int32, shape, 1)
    group, col = raw // LANES, raw % LANES
    place = (col % 4) * LANES + group * cells + col // 4
    return jnp.where(place == grouped, 1.0, 0.0).astype(BF16)


def row_windows(row, edge):
    lane = lane_index(row.shape)
    low = jnp.where(lane < DILATION, edge, turn(row, DILATION))
    high = jnp.where(lane >= LANES - DILATION, edge, turn(row, -DILATION))
    return (low, row, high)


class Framed:
    def __init__(self, body, low, high, top, bottom, step):
        self.rows = body.shape[1]
        self.refs = (body, low, high, top, bottom)
        self.step = step

    def windows(self, start, size):
        body, low, high, top, bottom = self.refs
        span = pl.ds(start, size)
        step = self.step
        edge_low = low[step, span, :].astype(F32)
        edge_high = turn(high[step, span, :].astype(F32), -DILATION)
        odd_slot = (lane_index(edge_low.shape) // DILATION) % 2 == 1
        edges = (
            jnp.where(odd_slot, edge_high, edge_low),
            jnp.where(odd_slot, edge_low, edge_high),
        )
        shift = (LANES - DILATION) - step * (2 * DILATION)
        for row in range(-1, self.rows + 1):
            if 0 <= row < self.rows:
                value = body[step, row, span, :].astype(F32)
                edge = turn(edges[row % 2], -DILATION * row)
            else:
                source = top if row < 0 else bottom
                value = source[step, span, :].astype(F32)
                edge = turn(source[source.shape[0] - 1, span, :].astype(F32), shift)
            yield row, row_windows(value, edge)


def depthwise_chunk(framed, start, size, taps, emit):
    sums = {}
    for row, windows in framed.windows(start, size):
        for above in range(3):
            target = row + 1 - above
            if not 0 <= target < framed.rows:
                continue
            for side in range(3):
                term = taps[3 * above + side] * windows[side]
                sums[target] = sums[target] + term if target in sums else term
        if row - 1 >= 0:
            emit(row - 1, sums.pop(row - 1))


def tap_columns(kernel_ref, start, size, flip):
    block = kernel_ref[pl.ds(start, size), :]
    order = [8 - tap if flip else tap for tap in range(9)]
    return [jnp.broadcast_to(block[:, tap : tap + 1], (size, LANES)) for tap in order]


def edge_columns(row_of, rows):
    low = high = None
    for row in range(rows):
        value = row_of(row)
        slot = lane_index(value.shape) // DILATION == row
        to_low = turn(value, DILATION * row)
        to_high = turn(value, DILATION * row + DILATION)
        low = jnp.where(slot, to_low, 0.0 if low is None else low)
        high = jnp.where(slot, to_high, 0.0 if high is None else high)
    return low.astype(BF16), high.astype(BF16)


def split_kernel(x_ref, rows_ref, low_ref, high_ref, flat):
    slices, channels, rows = x_ref.shape[:3]

    def one_slice(step, carry):
        flat[...] = x_ref[step].reshape(channels * rows, LANES).astype(F32)

        def row_of(row):
            value = flat[pl.ds(row, channels, stride=rows), :]
            rows_ref[step, row] = value.astype(BF16)
            return value

        low_ref[step], high_ref[step] = edge_columns(row_of, rows)
        return carry

    lax.fori_loop(0, slices, one_slice, 0)


def start_state(state_ref, kernel_ref, down_ref, table, start, taps_ref, down_back, flat, tap_rows):
    channels, rows = state_ref.shape[0], state_ref.shape[1]
    table[...] = regroup(rows // 4)
    flat[...] = state_ref[...].reshape(channels * rows, LANES).astype(F32)
    for phase in range(4):
        parts = [
            flat[pl.ds(row, channels, stride=rows), :].astype(BF16)
            for row in range(phase, rows, 4)
        ]
        start[phase * channels : (phase + 1) * channels, :] = mm(
            jnp.concatenate(parts, axis=1), table[...]
        )
    down_back[...] = down_ref[...].astype(F32).T.astype(BF16)
    tap_rows[...] = jnp.zeros_like(tap_rows)
    for above in range(3):
        tap_rows[3 * above : 3 * above + 3, :channels] = kernel_ref[above]
    taps_ref[...] = tap_rows[...].T[:channels]


def message_kernel(rows_ref, low_ref, high_ref, down_ref, up_ref):
    slices = rows_ref.shape[0]
    corner_down = corner_up = jnp.zeros(rows_ref.shape[2:], F32)
    for step in range(slices):
        down_ref[step] = rows_ref[step, rows_ref.shape[1] - 1]
        up_ref[step] = rows_ref[step, 0]
        base = 2 * DILATION * step
        low = low_ref[step].astype(F32)
        high = high_ref[step].astype(F32)
        slot = lane_index(low.shape) // DILATION
        corner_down = jnp.where(slot == 2 * step, turn(high, base + DILATION), corner_down)
        corner_down = jnp.where(
            slot == 2 * step + 1, turn(low, base + 2 * DILATION), corner_down
        )
        corner_up = jnp.where(slot == 2 * step, turn(high, base), corner_up)
        corner_up = jnp.where(slot == 2 * step + 1, turn(low, base + DILATION), corner_up)
    down_ref[slices] = corner_down.astype(BF16)
    up_ref[slices] = corner_up.astype(BF16)


def recur_kernel(
    ranks,
    scale,
    plan,
    x_ref,
    low_ref,
    high_ref,
    top_ref,
    bottom_ref,
    state_ref,
    kernel_ref,
    weight_ref,
    down_ref,
    *rest,
):
    cot_refs, rest = rest[:ranks], rest[ranks:]
    out_hbms, rest = rest[:ranks], rest[ranks:]
    rows_ref, edge_low_ref, edge_high_ref, grad_state_ref, packed_ref, taps_ref, *rest = rest
    keep, stack, state, conv, patch, down_sum, out_ref, dense, tap_sums, flat, *rest = rest
    table, down_back, tap_rows, cots, sems = rest
    start_state(
        state_ref, kernel_ref, down_ref, table, state, taps_ref, down_back, flat, tap_rows
    )
    for rank, cot_ref in enumerate(cot_refs):
        cots[rank] = cot_ref[...]
    slices, rows, channels = x_ref.shape[:3]
    blocks = x_ref.shape[0]
    down_sum[...] = jnp.zeros_like(down_sum)
    out_ref[:, :, LANES:, :] = jnp.zeros_like(out_ref[:, :, LANES:, :])
    size = CHUNK

    def slot_of(step):
        owner = jnp.clip(plan[step], 0, ranks - 1)
        return owner, jnp.clip(plan[blocks + step], 0, blocks - 1)

    def back_of(step):
        owner, dest = slot_of(step)
        return cots[jnp.bitwise_xor(owner, plan[2 * blocks]), dest]

    def forward_slice(step, outer):
        framed = Framed(x_ref, low_ref, high_ref, top_ref, bottom_ref, step)

        def conv_chunk(index, carry):
            start = pl.multiple_of(index * size, size)
            taps = tap_columns(taps_ref, start, size, False)

            def emit(row, value):
                conv[row, pl.ds(start, size), :] = value.astype(BF16)

            depthwise_chunk(framed, start, size, taps, emit)
            return carry

        lax.fori_loop(0, channels // size, conv_chunk, 0)
        wide = jnp.concatenate(
            [
                jnp.concatenate([conv[row] for row in range(phase, rows, 4)], axis=1)
                for phase in range(4)
            ],
            axis=0,
        )
        grouped = mm(wide, table[...]).astype(BF16)
        for phase in range(4):
            own = slice(phase * channels, (phase + 1) * channels)
            prior = state[own, :]
            stacked = jnp.concatenate([grouped[own], prior.astype(BF16)], axis=0)
            stack[step, phase] = stacked
            pre = mm(weight_ref[...], stacked)
            signed_update = jnp.tanh(0.5 * pre[:channels])
            signed_reset = jnp.tanh(0.5 * pre[channels : 2 * channels])
            update = 0.5 + 0.5 * signed_update
            stay = 0.5 - 0.5 * signed_update
            reset = 0.5 + 0.5 * signed_reset
            recurrent = pre[3 * channels :]
            candidate = jnp.tanh(pre[2 * channels : 3 * channels] + reset * recurrent)
            following = stay * prior + update * candidate
            state[own, :] = following
            act = update * (1.0 - candidate * candidate)
            act_reset = act * reset
            keep[step, 0, own, :] = (candidate - prior) * update * stay
            keep[step, 1, own, :] = act_reset * recurrent * (0.5 - 0.5 * signed_reset)
            keep[step, 2, own, :] = act
            keep[step, 3, own, :] = act_reset
            keep[step, 4, own, :] = stay
            rounded = following.astype(BF16).astype(F32)
            for col in range(4):
                patch[pl.ds(4 * phase + col, channels, stride=16), :] = rounded[
                    :, col * LANES : (col + 1) * LANES
                ]
        patched = patch[...].astype(BF16)
        owner, dest = slot_of(step)
        position = jnp.int32(0)
        for earlier in range(blocks):
            position += jnp.where((earlier < step) & (plan[earlier] == owner), 1, 0)
        position = jnp.minimum(position, out_ref.shape[1] - 1)
        distance = lax.rem(owner + ranks - plan[2 * blocks], ranks)
        block = mm(down_ref[...], patched).astype(BF16)
        label = (dest + 1).astype(F32)
        labels = jnp.full((LABEL_ROWS, LANES), label, F32).astype(BF16)
        out_ref[distance, position, :LANES, :] = block
        out_ref[distance, position, LANES:, :] = labels
        down_sum[...] += mm_back(back_of(step), patched)
        return outer

    lax.fori_loop(0, slices, forward_slice, 0)
    copies = [
        pltpu.make_async_copy(out_ref.at[rank], out_hbms[rank], sems.at[rank])
        for rank in range(ranks)
    ]
    for copy in copies:
        copy.start()
    carry = state
    carry[...] = jnp.zeros_like(carry)
    dense[...] = jnp.zeros_like(dense)
    tap_sums[...] = jnp.zeros_like(tap_sums)
    weight_back = weight_ref[...].astype(F32).T.astype(BF16)

    def backward_slice(index, outer):
        step = slices - 1 - index
        patch[...] = mm(down_back[...], back_of(step))
        flat_grads = []
        for phase in range(4):
            own = slice(phase * channels, (phase + 1) * channels)
            unpatched = jnp.concatenate(
                [patch[pl.ds(4 * phase + col, channels, stride=16), :] for col in range(4)],
                axis=1,
            )
            flow = carry[own, :] + unpatched
            delta = jnp.concatenate(
                [(flow * keep[step, part, own, :]).astype(BF16) for part in range(4)],
                axis=0,
            )
            reverse = mm(weight_back, delta)
            carry[own, :] = keep[step, 4, own, :] * flow + reverse[channels:]
            flat_grads.append(reverse[:channels].astype(BF16))
            dense[...] += lax.dot_general(
                delta, stack[step, phase], NT, preferred_element_type=F32
            )
        spread = mm_back(jnp.concatenate(flat_grads, axis=0), table[...])

        def row_of(row):
            group, phase = row // 4, row % 4
            value = spread[
                phase * channels : (phase + 1) * channels, group * LANES : (group + 1) * LANES
            ]
            rows_ref[step, row] = value.astype(BF16)
            return value

        edge_low_ref[step], edge_high_ref[step] = edge_columns(row_of, rows)
        framed = Framed(x_ref, low_ref, high_ref, top_ref, bottom_ref, step)

        def tap_chunk(index, loop_carry):
            start = pl.multiple_of(index * size, size)
            span = pl.ds(start, size)
            sums = [tap_sums[tap, span, :] for tap in range(9)]
            for row, windows in framed.windows(start, size):
                for above in range(3):
                    target = row + 1 - above
                    if not 0 <= target < rows:
                        continue
                    grad = rows_ref[step, target, span, :].astype(F32)
                    for side in range(3):
                        tap = 3 * above + side
                        sums[tap] = sums[tap] + grad * windows[side]
            for tap in range(9):
                tap_sums[tap, span, :] = sums[tap]
            return loop_carry

        lax.fori_loop(0, channels // size, tap_chunk, 0)
        return outer

    lax.fori_loop(0, slices, backward_slice, 0)
    remain = carry[...]
    total = None
    for _ in range(3):
        piece = remain.astype(BF16)
        remain = remain - piece.astype(F32)
        term = mm_back(piece, table[...])
        total = term if total is None else total + term
    for phase in range(4):
        for group in range(rows // 4):
            flat[pl.ds(4 * group + phase, channels, stride=rows), :] = total[
                phase * channels : (phase + 1) * channels,
                group * LANES : (group + 1) * LANES,
            ]
    grad_state_ref[...] = flat[...].reshape(channels, rows, LANES)
    lower = dense[2 * channels : 3 * channels, :]
    upper = dense[3 * channels :, :]
    merged = jnp.where(lane_index(lower.shape) < channels, lower, upper)
    gathered = jnp.zeros((channels, LANES), F32)
    for tap in range(9):
        column = jnp.sum(tap_sums[tap], axis=1, keepdims=True)
        gathered = jnp.where(lane_index(gathered.shape) == tap, column, gathered)
    tap_rows = jnp.concatenate(
        [gathered.T[:16], jnp.zeros((16, LANES - channels), F32)], axis=1
    )
    shares = packed_ref.shape[0]
    parts = [dense[: 2 * channels, :], merged, tap_rows]
    parts.append(jnp.zeros((8 * shares - 3 * channels - 16, LANES), F32))
    small = jnp.concatenate(parts, axis=0) * scale
    packed_ref[:, :16, :] = paired(small.reshape(shares, 8, LANES))
    for part in range(down_sum.shape[1] // LANES):
        value = down_sum[:, part * LANES : (part + 1) * LANES] * scale
        value = value.reshape((-1, packed_ref.shape[1] - 16, LANES))
        first = part * value.shape[0]
        packed_ref[first : first + value.shape[0], 16:, :] = value.astype(BF16)
    for copy in copies:
        copy.wait()


def paired(value):
    rounded = value.astype(BF16).astype(F32)
    return jnp.concatenate([rounded, value - rounded], axis=-2).astype(BF16)


def summed(pieces_ref):
    total = pieces_ref[0].astype(F32)
    for share in range(1, pieces_ref.shape[0]):
        total = total + pieces_ref[share].astype(F32)
    return total


def share_kernel(pieces_ref, out_ref):
    total = summed(pieces_ref)
    small = paired(total[:8] + total[8:16])
    down = total[16:].astype(BF16)
    for share in range(out_ref.shape[0]):
        out_ref[share, :16] = small
        out_ref[share, 16:] = down


def features_kernel(x_ref, low_ref, high_ref, top_ref, bottom_ref, taps_ref, out_ref, flat):
    slices, rows, channels = x_ref.shape[:3]
    size = CHUNK

    def one_slice(step, outer):
        framed = Framed(x_ref, low_ref, high_ref, top_ref, bottom_ref, step)

        def conv_chunk(index, carry):
            start = pl.multiple_of(index * size, size)
            taps = tap_columns(taps_ref, start, size, True)

            def emit(row, value):
                flat[pl.ds(start * rows + row, size, stride=rows), :] = value

            depthwise_chunk(framed, start, size, taps, emit)
            return carry

        lax.fori_loop(0, channels // size, conv_chunk, 0)
        out_ref[step] = flat[...].reshape(channels, rows, LANES).astype(BF16)
        return outer

    lax.fori_loop(0, slices, one_slice, 0)


def landing(arrived_refs, cart_ref):
    for dest in range(cart_ref.shape[0]):
        total = jnp.zeros(cart_ref.shape[1:], F32)
        for arrived_ref in arrived_refs:
            for slot in range(arrived_ref.shape[0]):
                label = arrived_ref[slot, LANES : LANES + LABEL_ROWS, :].astype(F32)[:1]
                value = arrived_ref[slot, :LANES, :].astype(F32)
                total = total + jnp.where(label == dest + 1, value, 0.0)
        cart_ref[dest] = total


def finish_kernel(spread_ref, *refs):
    *arrived_refs, gate_ref, cand_ref, recur_ref, taps_ref, down_ref, cart_ref = refs
    landing(arrived_refs, cart_ref)
    channels = cand_ref.shape[0]
    coarse_ch = down_ref.shape[0]
    shares = spread_ref.shape[0]
    small = spread_ref[:, :16, :].astype(F32)
    total = (small[:, :8] + small[:, 8:]).reshape(8 * shares, LANES)
    gate_ref[...] = total[: 2 * channels]
    cand_ref[...] = total[2 * channels : 3 * channels, :channels]
    recur_ref[...] = total[2 * channels : 3 * channels, channels:]
    for above in range(3):
        first = 3 * channels + 3 * above
        taps_ref[above] = total[first : first + 3, :channels]
    down = spread_ref[:, 16:, :].astype(F32).reshape(down_ref.shape[1] // LANES, coarse_ch, LANES)
    for part in range(down.shape[0]):
        down_ref[:, part * LANES : (part + 1) * LANES] = down[part]


def shifted(value, axis, distance, periodic):
    count = lax.axis_size(axis)
    pairs = [(i, i + 1) for i in range(count - 1)]
    if periodic:
        pairs.append((count - 1, 0))
    if distance < 0:
        pairs = [(target, source) for source, target in pairs]
    return lax.ppermute(value, axis, pairs)


def exchange(rows_array, edge_low, edge_high):
    slices, _, channels, _ = rows_array.shape
    low = shifted(edge_high, "azimuth", 1, True)
    high = shifted(edge_low, "azimuth", -1, True)
    message = jax.ShapeDtypeStruct((slices + 1, channels, LANES), BF16)
    down, up = pl.pallas_call(
        message_kernel,
        in_specs=[VMEM] * 3,
        out_specs=[VMEM] * 2,
        out_shape=[message] * 2,
        name="message",
        compiler_params=params(),
        cost_estimate=cost(1),
    )(rows_array, low, high)
    top = shifted(down, "range", 1, False)
    bottom = shifted(up, "range", -1, False)
    return (rows_array, low, high, top, bottom)


def params(mib=12):
    return pltpu.CompilerParams(vmem_limit_bytes=mib << 20)


def cost(mib, flops=1 << 20):
    return pl.CostEstimate(flops=flops, bytes_accessed=int(mib * (1 << 20)), transcendentals=0)


def on_device(
    features,
    state_init,
    kernel,
    gate_weight,
    cand_weight,
    recur_weight,
    down_weight,
    owner_map,
    dest_map,
    cart_cot,
):
    slices, channels, rows, cols = features.shape
    coarse_ch = down_weight.shape[0]
    ranks = lax.axis_size("range")
    shares = ranks * lax.axis_size("azimuth")
    blocks = owner_map.shape[2]
    capacity = blocks // 2
    assert cols == LANES and rows * DILATION == LANES and blocks == slices
    scale = 1.0 / math.sqrt(slices * rows * cols * shares)
    me = lax.axis_index("range").astype(jnp.int32)
    plan = jnp.concatenate(
        [owner_map.reshape(blocks), dest_map.reshape(blocks), me.reshape(1)]
    )
    empty = jnp.zeros(cand_weight.shape, BF16)
    weights = jnp.concatenate(
        [
            gate_weight,
            jnp.concatenate([cand_weight, empty], axis=1),
            jnp.concatenate([empty, recur_weight], axis=1),
        ],
        axis=0,
    )
    flat_scratch = pltpu.VMEM((channels * rows, LANES), F32)
    row_shape = jax.ShapeDtypeStruct((slices, rows, channels, LANES), BF16)
    edge_shape = jax.ShapeDtypeStruct((slices, channels, LANES), BF16)
    cot_shape = jax.ShapeDtypeStruct((blocks, coarse_ch, LANES), BF16)
    group = (4 * channels, 4 * LANES)
    out_blocks = jax.ShapeDtypeStruct((capacity, coarse_ch + LABEL_ROWS, LANES), BF16)
    down_rows = 16 * channels * coarse_ch // (LANES * shares)
    packed_shape = jax.ShapeDtypeStruct((shares, 16 + down_rows, LANES), BF16)
    everyone = ("range", "azimuth")

    pieces = {0: cart_cot.reshape(cot_shape.shape)}
    gap = ranks // 2
    far = lax.ppermute(pieces[0], "range", [(i, i ^ gap) for i in range(ranks)])
    arranged, edge_low, edge_high = pl.pallas_call(
        split_kernel,
        in_specs=[VMEM],
        out_specs=[VMEM] * 3,
        out_shape=[row_shape, edge_shape, edge_shape],
        scratch_shapes=[flat_scratch],
        name="split",
        compiler_params=params(),
        cost_estimate=cost(3),
    )(features)
    frame = exchange(arranged, edge_low, edge_high)
    pieces[gap] = far
    gap //= 2
    while gap:
        for rank in list(pieces):
            pieces[rank ^ gap] = lax.ppermute(
                pieces[rank], "range", [(i, i ^ gap) for i in range(ranks)]
            )
        gap //= 2
    *outgoing, rows_grad, low_grad, high_grad, grad_state, packed, taps = pl.pallas_call(
        functools.partial(recur_kernel, ranks, scale),
        in_specs=[SMEM] + [VMEM] * (9 + ranks),
        out_specs=[HBM] * ranks + [VMEM] * 6,
        out_shape=[out_blocks] * ranks
        + [
            row_shape,
            edge_shape,
            edge_shape,
            jax.ShapeDtypeStruct((channels, rows, LANES), F32),
            packed_shape,
            jax.ShapeDtypeStruct((channels, 16), F32),
        ],
        scratch_shapes=[
            pltpu.VMEM((slices, 5) + group, F32),
            pltpu.VMEM((slices, 4, 2 * channels, 4 * LANES), BF16),
            pltpu.VMEM(group, F32),
            pltpu.VMEM((rows, channels, LANES), BF16),
            pltpu.VMEM((16 * channels, LANES), F32),
            pltpu.VMEM(down_weight.shape, F32),
            pltpu.VMEM((ranks,) + out_blocks.shape, BF16),
            pltpu.VMEM((4 * channels, 2 * channels), F32),
            pltpu.VMEM((9, channels, LANES), F32),
            flat_scratch,
            pltpu.VMEM((rows // 4 * LANES, 4 * LANES), BF16),
            pltpu.VMEM(down_weight.shape[::-1], BF16),
            pltpu.VMEM((16, LANES), F32),
            pltpu.VMEM((ranks,) + cot_shape.shape, BF16),
            pltpu.SemaphoreType.DMA((ranks,)),
        ],
        name="recur",
        compiler_params=params(28),
        cost_estimate=cost(16, 1 << 31),
    )(
        plan,
        *frame,
        state_init,
        kernel.transpose(1, 2, 0),
        weights,
        down_weight,
        *[pieces[rank] for rank in range(ranks)],
    )

    pieces = lax.all_to_all(packed, everyone, 0, 0, tiled=True)
    frame_grad = exchange(rows_grad, low_grad, high_grad)
    arrived = [outgoing[0]] + [
        lax.ppermute(outgoing[rank], "range", [(i, (i + rank) % ranks) for i in range(ranks)])
        for rank in range(1, ranks)
    ]
    shared = pl.pallas_call(
        share_kernel,
        in_specs=[VMEM],
        out_specs=VMEM,
        out_shape=packed_shape,
        name="share",
        compiler_params=params(),
        cost_estimate=cost(1),
    )(pieces)
    spread = lax.all_to_all(shared, everyone, 0, 0, tiled=True)
    grad_features = pl.pallas_call(
        features_kernel,
        in_specs=[VMEM] * 6,
        out_specs=VMEM,
        out_shape=jax.ShapeDtypeStruct(features.shape, BF16),
        scratch_shapes=[flat_scratch],
        name="features",
        compiler_params=params(),
        cost_estimate=cost(4, 1 << 25),
    )(*frame_grad, taps)
    grad_gate, grad_cand, grad_recur, grad_taps, grad_down, cartesian = pl.pallas_call(
        finish_kernel,
        in_specs=[VMEM] * (1 + ranks),
        out_specs=[VMEM] * 6,
        out_shape=[
            jax.ShapeDtypeStruct(gate_weight.shape, F32),
            jax.ShapeDtypeStruct(cand_weight.shape, F32),
            jax.ShapeDtypeStruct(recur_weight.shape, F32),
            jax.ShapeDtypeStruct((3, 3, channels), F32),
            jax.ShapeDtypeStruct(down_weight.shape, F32),
            jax.ShapeDtypeStruct(cot_shape.shape, F32),
        ],
        name="finish",
        compiler_params=params(),
        cost_estimate=cost(1),
    )(spread, *arrived)
    return (
        cartesian.reshape(cart_cot.shape),
        grad_features,
        grad_state,
        grad_taps.transpose(2, 0, 1),
        grad_gate,
        grad_cand,
        grad_recur,
        grad_down,
    )


def solution(mesh):
    placed = (
        P(None, None, "range", "azimuth"),
        P(None, "range", "azimuth"),
        P(),
        P(),
        P(),
        P(),
        P(),
        P("range", "azimuth", None),
        P("range", "azimuth", None),
        P("range", "azimuth", None, None, None),
    )
    return jax.shard_map(
        on_device,
        mesh=mesh,
        in_specs=placed,
        out_specs=(
            P("range", "azimuth", None, None, None),
            P(None, None, "range", "azimuth"),
            P(None, "range", "azimuth"),
            P(),
            P(),
            P(),
            P(),
            P(),
        ),
        check_vma=False,
    )
```

```python
import functools
import math

import jax
import jax.numpy as jnp
from jax import lax
from jax.experimental import pallas as pl
from jax.experimental.pallas import tpu as pltpu
from jax.sharding import PartitionSpec as P


DILATION = 8
LANES = 128
LABEL_ROWS = 16
CHUNK = 16
F32 = jnp.float32
BF16 = jnp.bfloat16
NT = (((1,), (1,)), ((), ()))
VMEM = pl.BlockSpec(memory_space=pltpu.VMEM)
HBM = pl.BlockSpec(memory_space=pltpu.HBM)
SMEM = pl.BlockSpec(memory_space=pltpu.SMEM)


def mm(left, right):
    return jnp.dot(left, right, preferred_element_type=F32)


def mm_back(left, right):
    return lax.dot_general(left, right, NT, preferred_element_type=F32)


def turn(value, shift):
    if isinstance(shift, int):
        shift = shift % LANES
        if shift == 0:
            return value
    return pltpu.roll(value, shift, 1)


def lane_index(shape):
    return lax.broadcasted_iota(jnp.int32, shape, len(shape) - 1)


def regroup(row_groups):
    cells = LANES // row_groups
    shape = (row_groups * LANES, 4 * LANES)
    raw = lax.broadcasted_iota(jnp.int32, shape, 0)
    grouped = lax.broadcasted_iota(jnp.int32, shape, 1)
    group, col = raw // LANES, raw % LANES
    place = (col % 4) * LANES + group * cells + col // 4
    return jnp.where(place == grouped, 1.0, 0.0).astype(BF16)


def row_windows(row, edge):
    lane = lane_index(row.shape)
    low = jnp.where(lane < DILATION, edge, turn(row, DILATION))
    high = jnp.where(lane >= LANES - DILATION, edge, turn(row, -DILATION))
    return (low, row, high)


class Framed:
    def __init__(self, body, low, high, top, bottom, step):
        self.rows = body.shape[1]
        self.refs = (body, low, high, top, bottom)
        self.step = step

    def windows(self, start, size):
        body, low, high, top, bottom = self.refs
        span = pl.ds(start, size)
        step = self.step
        edge_low = low[step, span, :].astype(F32)
        edge_high = turn(high[step, span, :].astype(F32), -DILATION)
        odd_slot = (lane_index(edge_low.shape) // DILATION) % 2 == 1
        edges = (
            jnp.where(odd_slot, edge_high, edge_low),
            jnp.where(odd_slot, edge_low, edge_high),
        )
        shift = (LANES - DILATION) - step * (2 * DILATION)
        for row in range(-1, self.rows + 1):
            if 0 <= row < self.rows:
                value = body[step, row, span, :].astype(F32)
                edge = turn(edges[row % 2], -DILATION * row)
            else:
                source = top if row < 0 else bottom
                value = source[step, span, :].astype(F32)
                edge = turn(source[source.shape[0] - 1, span, :].astype(F32), shift)
            yield row, row_windows(value, edge)


def depthwise_chunk(framed, start, size, taps, emit, save=None):
    sums = {}
    for row, windows in framed.windows(start, size):
        if save is not None:
            save(row, windows)
        for above in range(3):
            target = row + 1 - above
            if not 0 <= target < framed.rows:
                continue
            for side in range(3):
                term = taps[3 * above + side] * windows[side]
                sums[target] = sums[target] + term if target in sums else term
        if row - 1 >= 0:
            emit(row - 1, sums.pop(row - 1))


def tap_columns(kernel_ref, start, size, flip):
    block = kernel_ref[pl.ds(start, size), :]
    order = [8 - tap if flip else tap for tap in range(9)]
    return [jnp.broadcast_to(block[:, tap : tap + 1], (size, LANES)) for tap in order]


def edge_columns(row_of, rows):
    low = high = None
    for row in range(rows):
        value = row_of(row)
        slot = lane_index(value.shape) // DILATION == row
        to_low = turn(value, DILATION * row)
        to_high = turn(value, DILATION * row + DILATION)
        low = jnp.where(slot, to_low, 0.0 if low is None else low)
        high = jnp.where(slot, to_high, 0.0 if high is None else high)
    return low.astype(BF16), high.astype(BF16)


def split_kernel(x_ref, rows_ref, low_ref, high_ref, flat):
    slices, channels, rows = x_ref.shape[:3]

    def one_slice(step, carry):
        flat[...] = x_ref[step].reshape(channels * rows, LANES).astype(F32)

        def row_of(row):
            value = flat[pl.ds(row, channels, stride=rows), :]
            rows_ref[step, row] = value.astype(BF16)
            return value

        low_ref[step], high_ref[step] = edge_columns(row_of, rows)
        return carry

    lax.fori_loop(0, slices, one_slice, 0)


def start_state(state_ref, kernel_ref, down_ref, table, start, taps_ref, down_back, flat, tap_rows):
    channels, rows = state_ref.shape[0], state_ref.shape[1]
    table[...] = regroup(rows // 4)
    flat[...] = state_ref[...].reshape(channels * rows, LANES).astype(F32)
    for phase in range(4):
        parts = [
            flat[pl.ds(row, channels, stride=rows), :].astype(BF16)
            for row in range(phase, rows, 4)
        ]
        start[phase * channels : (phase + 1) * channels, :] = mm(
            jnp.concatenate(parts, axis=1), table[...]
        )
    down_back[...] = down_ref[...].astype(F32).T.astype(BF16)
    tap_rows[...] = jnp.zeros_like(tap_rows)
    for above in range(3):
        tap_rows[3 * above : 3 * above + 3, :channels] = kernel_ref[above]
    taps_ref[...] = tap_rows[...].T[:channels]


def message_kernel(rows_ref, low_ref, high_ref, down_ref, up_ref):
    slices = rows_ref.shape[0]
    corner_down = corner_up = jnp.zeros(rows_ref.shape[2:], F32)
    for step in range(slices):
        down_ref[step] = rows_ref[step, rows_ref.shape[1] - 1]
        up_ref[step] = rows_ref[step, 0]
        base = 2 * DILATION * step
        low = low_ref[step].astype(F32)
        high = high_ref[step].astype(F32)
        slot = lane_index(low.shape) // DILATION
        corner_down = jnp.where(slot == 2 * step, turn(high, base + DILATION), corner_down)
        corner_down = jnp.where(
            slot == 2 * step + 1, turn(low, base + 2 * DILATION), corner_down
        )
        corner_up = jnp.where(slot == 2 * step, turn(high, base), corner_up)
        corner_up = jnp.where(slot == 2 * step + 1, turn(low, base + DILATION), corner_up)
    down_ref[slices] = corner_down.astype(BF16)
    up_ref[slices] = corner_up.astype(BF16)


def recur_kernel(
    ranks,
    scale,
    plan,
    x_ref,
    low_ref,
    high_ref,
    top_ref,
    bottom_ref,
    state_ref,
    kernel_ref,
    weight_ref,
    down_ref,
    *rest,
):
    cot_refs, rest = rest[:ranks], rest[ranks:]
    out_hbms, rest = rest[:ranks], rest[ranks:]
    rows_ref, edge_low_ref, edge_high_ref, grad_state_ref, packed_ref, taps_ref, *rest = rest
    keep, stack, state, conv, patch, down_sum, out_ref, dense, tap_sums, flat, *rest = rest
    table, down_back, tap_rows, cots, seen, wide_grad, sems = rest
    start_state(
        state_ref, kernel_ref, down_ref, table, state, taps_ref, down_back, flat, tap_rows
    )
    for rank, cot_ref in enumerate(cot_refs):
        cots[rank] = cot_ref[...]
    slices, rows, channels = x_ref.shape[:3]
    blocks = x_ref.shape[0]
    down_sum[...] = jnp.zeros_like(down_sum)
    out_ref[:, :, LANES:, :] = jnp.zeros_like(out_ref[:, :, LANES:, :])
    size = CHUNK
    gate_rows = lax.broadcasted_iota(jnp.int32, weight_ref.shape, 0) < 2 * channels
    weight = weight_ref[...].astype(F32)
    half_weight = jnp.where(gate_rows, 0.5 * weight, weight).astype(BF16)

    def slot_of(step):
        owner = jnp.clip(plan[step], 0, ranks - 1)
        return owner, jnp.clip(plan[blocks + step], 0, blocks - 1)

    def back_of(step):
        owner, dest = slot_of(step)
        return cots[jnp.bitwise_xor(owner, plan[2 * blocks]), dest]

    def forward_slice(step, outer):
        framed = Framed(x_ref, low_ref, high_ref, top_ref, bottom_ref, step)

        def conv_chunk(index, carry):
            start = pl.multiple_of(index * size, size)
            taps = tap_columns(taps_ref, start, size, False)

            def emit(row, value):
                conv[row, pl.ds(start, size), :] = value.astype(BF16)

            def save(row, windows):
                lanes = slice((row + 1) * LANES, (row + 2) * LANES)
                for side in range(3):
                    span = pl.ds(side * channels + start, size)
                    seen[step, span, lanes] = windows[side].astype(BF16)

            depthwise_chunk(framed, start, size, taps, emit, save)
            return carry

        lax.fori_loop(0, channels // size, conv_chunk, 0)
        wide = jnp.concatenate(
            [
                jnp.concatenate([conv[row] for row in range(phase, rows, 4)], axis=1)
                for phase in range(4)
            ],
            axis=0,
        )
        grouped = mm(wide, table[...]).astype(BF16)
        for phase in range(4):
            stack[step, phase, :channels, :] = grouped[phase * channels : (phase + 1) * channels]
        for phase in range(4):
            own = slice(phase * channels, (phase + 1) * channels)
            for col in range(4):
                part = slice(col * LANES, (col + 1) * LANES)
                prior = state[own, part]
                stack[step, phase, channels:, part] = prior.astype(BF16)
                pre = mm(half_weight, stack[step, phase, :, part])
                half_update = 0.5 * jnp.tanh(pre[:channels])
                half_reset = 0.5 * jnp.tanh(pre[channels : 2 * channels])
                update = 0.5 + half_update
                stay = 0.5 - half_update
                reset = 0.5 + half_reset
                recurrent = reset * pre[3 * channels :]
                candidate = jnp.tanh(pre[2 * channels : 3 * channels] + recurrent)
                step_by = update * (candidate - prior)
                following = prior + step_by
                state[own, part] = following
                patch[pl.ds(4 * phase + col, channels, stride=16), :] = following
                act = update * (1.0 - candidate * candidate)
                keep[step, 0, own, part] = step_by * stay
                keep[step, 1, own, part] = act * recurrent * (0.5 - half_reset)
                keep[step, 2, own, part] = act
                keep[step, 3, own, part] = act * reset
                keep[step, 4, own, part] = stay
        patched = patch[...].astype(BF16)
        owner, dest = slot_of(step)
        position = jnp.int32(0)
        for earlier in range(blocks):
            position += jnp.where((earlier < step) & (plan[earlier] == owner), 1, 0)
        position = jnp.minimum(position, out_ref.shape[1] - 1)
        distance = lax.rem(owner + ranks - plan[2 * blocks], ranks)
        block = mm(down_ref[...], patched).astype(BF16)
        label = (dest + 1).astype(F32)
        labels = jnp.full((LABEL_ROWS, LANES), label, F32).astype(BF16)
        out_ref[distance, position, :LANES, :] = block
        out_ref[distance, position, LANES:, :] = labels
        down_sum[...] += mm_back(back_of(step), patched)
        return outer

    lax.fori_loop(0, slices, forward_slice, 0)
    copies = [
        pltpu.make_async_copy(out_ref.at[rank], out_hbms[rank], sems.at[rank])
        for rank in range(ranks)
    ]
    for copy in copies:
        copy.start()
    carry = state
    carry[...] = jnp.zeros_like(carry)
    dense[...] = jnp.zeros_like(dense)
    tap_sums[...] = jnp.zeros_like(tap_sums)
    weight_back = weight_ref[...].astype(F32).T.astype(BF16)

    def backward_slice(index, outer):
        step = slices - 1 - index
        patch[...] = mm(down_back[...], back_of(step))
        flat_grads = []
        for phase in range(4):
            own = slice(phase * channels, (phase + 1) * channels)
            unpatched = jnp.concatenate(
                [patch[pl.ds(4 * phase + col, channels, stride=16), :] for col in range(4)],
                axis=1,
            )
            flow = carry[own, :] + unpatched
            delta = jnp.concatenate(
                [(flow * keep[step, part, own, :]).astype(BF16) for part in range(4)],
                axis=0,
            )
            reverse = mm(weight_back, delta)
            carry[own, :] = keep[step, 4, own, :] * flow + reverse[channels:]
            flat_grads.append(reverse[:channels].astype(BF16))
            dense[...] += lax.dot_general(
                delta, stack[step, phase], NT, preferred_element_type=F32
            )
        spread = mm_back(jnp.concatenate(flat_grads, axis=0), table[...])

        def row_of(row):
            group, phase = row // 4, row % 4
            value = spread[
                phase * channels : (phase + 1) * channels, group * LANES : (group + 1) * LANES
            ]
            rounded = value.astype(BF16)
            rows_ref[step, row] = rounded
            wide_grad[:, row * LANES : (row + 1) * LANES] = rounded
            return value

        edge_low_ref[step], edge_high_ref[step] = edge_columns(row_of, rows)
        for above in range(3):
            lanes = slice(above * LANES, (above + rows) * LANES)
            tap_sums[above] += mm_back(wide_grad[...], seen[step, :, lanes])
        return outer

    lax.fori_loop(0, slices, backward_slice, 0)
    remain = carry[...]
    total = None
    for _ in range(3):
        piece = remain.astype(BF16)
        remain = remain - piece.astype(F32)
        term = mm_back(piece, table[...])
        total = term if total is None else total + term
    for phase in range(4):
        for group in range(rows // 4):
            flat[pl.ds(4 * group + phase, channels, stride=rows), :] = total[
                phase * channels : (phase + 1) * channels,
                group * LANES : (group + 1) * LANES,
            ]
    grad_state_ref[...] = flat[...].reshape(channels, rows, LANES)
    lower = dense[2 * channels : 3 * channels, :]
    upper = dense[3 * channels :, :]
    merged = jnp.where(lane_index(lower.shape) < channels, lower, upper)
    gathered = jnp.zeros((channels, LANES), F32)
    for tap in range(9):
        above, side = tap // 3, tap % 3
        block = tap_sums[above]
        own = lax.broadcasted_iota(jnp.int32, block.shape, 0) + side * channels
        same = own == lane_index(block.shape)
        column = jnp.sum(jnp.where(same, block, 0.0), axis=1, keepdims=True)
        gathered = jnp.where(lane_index(gathered.shape) == tap, column, gathered)
    tap_rows = jnp.concatenate(
        [gathered.T[:16], jnp.zeros((16, LANES - channels), F32)], axis=1
    )
    shares = packed_ref.shape[0]
    parts = [dense[: 2 * channels, :], merged, tap_rows]
    parts.append(jnp.zeros((8 * shares - 3 * channels - 16, LANES), F32))
    small = jnp.concatenate(parts, axis=0) * scale
    down_rows = packed_ref.shape[1] - 8
    packed_ref[:, down_rows:, :] = small.reshape(shares, 8, LANES).astype(BF16)
    for part in range(down_sum.shape[1] // LANES):
        value = down_sum[:, part * LANES : (part + 1) * LANES] * scale
        value = value.reshape((-1, down_rows, LANES))
        first = part * value.shape[0]
        packed_ref[first : first + value.shape[0], :down_rows, :] = value.astype(BF16)
    for copy in copies:
        copy.wait()


def share_kernel(pieces_ref, out_ref):
    total = pieces_ref[0].astype(F32)
    for share in range(1, pieces_ref.shape[0]):
        total = total + pieces_ref[share].astype(F32)
    total = total.astype(BF16)
    for share in range(out_ref.shape[0]):
        out_ref[share] = total


def features_kernel(x_ref, low_ref, high_ref, top_ref, bottom_ref, taps_ref, out_ref, flat):
    slices, rows, channels = x_ref.shape[:3]
    size = CHUNK

    def one_slice(step, outer):
        framed = Framed(x_ref, low_ref, high_ref, top_ref, bottom_ref, step)

        def conv_chunk(index, carry):
            start = pl.multiple_of(index * size, size)
            taps = tap_columns(taps_ref, start, size, True)

            def emit(row, value):
                flat[pl.ds(start * rows + row, size, stride=rows), :] = value

            depthwise_chunk(framed, start, size, taps, emit)
            return carry

        lax.fori_loop(0, channels // size, conv_chunk, 0)
        out_ref[step] = flat[...].reshape(channels, rows, LANES).astype(BF16)
        return outer

    lax.fori_loop(0, slices, one_slice, 0)


def landing(arrived_refs, cart_ref):
    for dest in range(cart_ref.shape[0]):
        total = jnp.zeros(cart_ref.shape[1:], F32)
        for arrived_ref in arrived_refs:
            for slot in range(arrived_ref.shape[0]):
                label = arrived_ref[slot, LANES : LANES + LABEL_ROWS, :].astype(F32)[:1]
                value = arrived_ref[slot, :LANES, :].astype(F32)
                total = total + jnp.where(label == dest + 1, value, 0.0)
        cart_ref[dest] = total


def finish_kernel(spread_ref, *refs):
    *arrived_refs, gate_ref, cand_ref, recur_ref, taps_ref, down_ref, cart_ref = refs
    landing(arrived_refs, cart_ref)
    channels = cand_ref.shape[0]
    coarse_ch = down_ref.shape[0]
    shares = spread_ref.shape[0]
    down_rows = spread_ref.shape[1] - 8
    total = spread_ref[:, down_rows:, :].astype(F32).reshape(8 * shares, LANES)
    gate_ref[...] = total[: 2 * channels]
    cand_ref[...] = total[2 * channels : 3 * channels, :channels]
    recur_ref[...] = total[2 * channels : 3 * channels, channels:]
    for above in range(3):
        first = 3 * channels + 3 * above
        taps_ref[above] = total[first : first + 3, :channels]
    down = spread_ref[:, :down_rows, :].astype(F32).reshape(down_ref.shape[1] // LANES, coarse_ch, LANES)
    for part in range(down.shape[0]):
        down_ref[:, part * LANES : (part + 1) * LANES] = down[part]


def shifted(value, axis, distance, periodic):
    count = lax.axis_size(axis)
    pairs = [(i, i + 1) for i in range(count - 1)]
    if periodic:
        pairs.append((count - 1, 0))
    if distance < 0:
        pairs = [(target, source) for source, target in pairs]
    return lax.ppermute(value, axis, pairs)


def exchange(rows_array, edge_low, edge_high):
    slices, _, channels, _ = rows_array.shape
    low = shifted(edge_high, "azimuth", 1, True)
    high = shifted(edge_low, "azimuth", -1, True)
    message = jax.ShapeDtypeStruct((slices + 1, channels, LANES), BF16)
    down, up = pl.pallas_call(
        message_kernel,
        in_specs=[VMEM] * 3,
        out_specs=[VMEM] * 2,
        out_shape=[message] * 2,
        name="message",
        compiler_params=params(),
        cost_estimate=cost(1),
    )(rows_array, low, high)
    top = shifted(down, "range", 1, False)
    bottom = shifted(up, "range", -1, False)
    return (rows_array, low, high, top, bottom)


def params(mib=12):
    return pltpu.CompilerParams(vmem_limit_bytes=mib << 20)


def cost(mib, flops=1 << 20):
    return pl.CostEstimate(flops=flops, bytes_accessed=int(mib * (1 << 20)), transcendentals=0)


def on_device(
    features,
    state_init,
    kernel,
    gate_weight,
    cand_weight,
    recur_weight,
    down_weight,
    owner_map,
    dest_map,
    cart_cot,
):
    slices, channels, rows, cols = features.shape
    coarse_ch = down_weight.shape[0]
    ranks = lax.axis_size("range")
    shares = ranks * lax.axis_size("azimuth")
    blocks = owner_map.shape[2]
    capacity = blocks // 2
    assert cols == LANES and rows * DILATION == LANES and blocks == slices
    scale = 1.0 / math.sqrt(slices * rows * cols * shares)
    me = lax.axis_index("range").astype(jnp.int32)
    plan = jnp.concatenate(
        [owner_map.reshape(blocks), dest_map.reshape(blocks), me.reshape(1)]
    )
    empty = jnp.zeros(cand_weight.shape, BF16)
    weights = jnp.concatenate(
        [
            gate_weight,
            jnp.concatenate([cand_weight, empty], axis=1),
            jnp.concatenate([empty, recur_weight], axis=1),
        ],
        axis=0,
    )
    flat_scratch = pltpu.VMEM((channels * rows, LANES), F32)
    row_shape = jax.ShapeDtypeStruct((slices, rows, channels, LANES), BF16)
    edge_shape = jax.ShapeDtypeStruct((slices, channels, LANES), BF16)
    cot_shape = jax.ShapeDtypeStruct((blocks, coarse_ch, LANES), BF16)
    group = (4 * channels, 4 * LANES)
    out_blocks = jax.ShapeDtypeStruct((capacity, coarse_ch + LABEL_ROWS, LANES), BF16)
    down_rows = 16 * channels * coarse_ch // (LANES * shares)
    packed_shape = jax.ShapeDtypeStruct((shares, 8 + down_rows, LANES), BF16)
    everyone = ("range", "azimuth")

    pieces = {0: cart_cot.reshape(cot_shape.shape)}
    gap = ranks // 2
    far = lax.ppermute(pieces[0], "range", [(i, i ^ gap) for i in range(ranks)])
    arranged, edge_low, edge_high = pl.pallas_call(
        split_kernel,
        in_specs=[VMEM],
        out_specs=[VMEM] * 3,
        out_shape=[row_shape, edge_shape, edge_shape],
        scratch_shapes=[flat_scratch],
        name="split",
        compiler_params=params(),
        cost_estimate=cost(3),
    )(features)
    frame = exchange(arranged, edge_low, edge_high)
    pieces[gap] = far
    gap //= 2
    while gap:
        for rank in list(pieces):
            pieces[rank ^ gap] = lax.ppermute(
                pieces[rank], "range", [(i, i ^ gap) for i in range(ranks)]
            )
        gap //= 2
    *outgoing, rows_grad, low_grad, high_grad, grad_state, packed, taps = pl.pallas_call(
        functools.partial(recur_kernel, ranks, scale),
        in_specs=[SMEM] + [VMEM] * (9 + ranks),
        out_specs=[HBM] * ranks + [VMEM] * 6,
        out_shape=[out_blocks] * ranks
        + [
            row_shape,
            edge_shape,
            edge_shape,
            jax.ShapeDtypeStruct((channels, rows, LANES), F32),
            packed_shape,
            jax.ShapeDtypeStruct((channels, 16), F32),
        ],
        scratch_shapes=[
            pltpu.VMEM((slices, 5) + group, F32),
            pltpu.VMEM((slices, 4, 2 * channels, 4 * LANES), BF16),
            pltpu.VMEM(group, F32),
            pltpu.VMEM((rows, channels, LANES), BF16),
            pltpu.VMEM((16 * channels, LANES), F32),
            pltpu.VMEM(down_weight.shape, F32),
            pltpu.VMEM((ranks,) + out_blocks.shape, BF16),
            pltpu.VMEM((4 * channels, 2 * channels), F32),
            pltpu.VMEM((3, channels, 3 * channels), F32),
            flat_scratch,
            pltpu.VMEM((rows // 4 * LANES, 4 * LANES), BF16),
            pltpu.VMEM(down_weight.shape[::-1], BF16),
            pltpu.VMEM((16, LANES), F32),
            pltpu.VMEM((ranks,) + cot_shape.shape, BF16),
            pltpu.VMEM((slices, 3 * channels, (rows + 2) * LANES), BF16),
            pltpu.VMEM((channels, rows * LANES), BF16),
            pltpu.SemaphoreType.DMA((ranks,)),
        ],
        name="recur",
        compiler_params=params(32),
        cost_estimate=cost(16, 1 << 31),
    )(
        plan,
        *frame,
        state_init,
        kernel.transpose(1, 2, 0),
        weights,
        down_weight,
        *[pieces[rank] for rank in range(ranks)],
    )

    pieces = lax.all_to_all(packed, everyone, 0, 0, tiled=True)
    frame_grad = exchange(rows_grad, low_grad, high_grad)
    arrived = [outgoing[0]] + [
        lax.ppermute(outgoing[rank], "range", [(i, (i + rank) % ranks) for i in range(ranks)])
        for rank in range(1, ranks)
    ]
    shared = pl.pallas_call(
        share_kernel,
        in_specs=[VMEM],
        out_specs=VMEM,
        out_shape=packed_shape,
        name="share",
        compiler_params=params(),
        cost_estimate=cost(1),
    )(pieces)
    spread = lax.all_to_all(shared, everyone, 0, 0, tiled=True)
    grad_features = pl.pallas_call(
        features_kernel,
        in_specs=[VMEM] * 6,
        out_specs=VMEM,
        out_shape=jax.ShapeDtypeStruct(features.shape, BF16),
        scratch_shapes=[flat_scratch],
        name="features",
        compiler_params=params(),
        cost_estimate=cost(4, 1 << 25),
    )(*frame_grad, taps)
    grad_gate, grad_cand, grad_recur, grad_taps, grad_down, cartesian = pl.pallas_call(
        finish_kernel,
        in_specs=[VMEM] * (1 + ranks),
        out_specs=[VMEM] * 6,
        out_shape=[
            jax.ShapeDtypeStruct(gate_weight.shape, F32),
            jax.ShapeDtypeStruct(cand_weight.shape, F32),
            jax.ShapeDtypeStruct(recur_weight.shape, F32),
            jax.ShapeDtypeStruct((3, 3, channels), F32),
            jax.ShapeDtypeStruct(down_weight.shape, F32),
            jax.ShapeDtypeStruct(cot_shape.shape, F32),
        ],
        name="finish",
        compiler_params=params(),
        cost_estimate=cost(1),
    )(spread, *arrived)
    return (
        cartesian.reshape(cart_cot.shape),
        grad_features,
        grad_state,
        grad_taps.transpose(2, 0, 1),
        grad_gate,
        grad_cand,
        grad_recur,
        grad_down,
    )


def solution(mesh):
    placed = (
        P(None, None, "range", "azimuth"),
        P(None, "range", "azimuth"),
        P(),
        P(),
        P(),
        P(),
        P(),
        P("range", "azimuth", None),
        P("range", "azimuth", None),
        P("range", "azimuth", None, None, None),
    )
    return jax.shard_map(
        on_device,
        mesh=mesh,
        in_specs=placed,
        out_specs=(
            P("range", "azimuth", None, None, None),
            P(None, None, "range", "azimuth"),
            P(None, "range", "azimuth"),
            P(),
            P(),
            P(),
            P(),
            P(),
        ),
        check_vma=False,
    )
```
